512 devices in a mesh: row: 16 (over y, z_hi), col: 32 (over z_lo, x, core).
Axes of the slice: x: 4, y: 4, z: 16 (z_hi: 4, z_lo: 4; z = z_hi * 4 + z_lo), core: 2. Of those that a mesh axis runs over, the one named last changes fastest.
Arguments:
- activations: bfloat16 [512, 28672], P('col', 'row'), may hold values from -6 to 6
- act_basis: bfloat16 [28672, 28672], P('row', 'col'), may hold values from -0.03125 to 0.03125
- out_grads: bfloat16 [512, 8192], P('row', 'col'), may hold values from -0.375 to 0.375
- grad_basis: bfloat16 [8192, 8192], P('col', 'row'), may hold values from -0.0625 to 0.0625
Outputs:
- eigen_lambda: bfloat16 [8192, 28672], P('row', 'col')
The draws below stay inside these ranges and needn't reach their ends.
All inputs are finite; a program needn't handle non-finite values.
Results may differ from the reference program's by a relative error of at most 0.0058.
Values may be sent and summed in bfloat16 or wider, within the bound.
A program may use at most 64 MiB of HBM per device.

```python
import jax
import jax.numpy as jnp
from jax import lax

IN = 28672
OUT = 8192
SEQS = 2
SEQ_LEN = 256
TOK = 512


def steps_of(stream_key, shape, shards, smallest, largest):
    def one(dim, parts):
        draws = jax.random.uniform(jax.random.fold_in(jax.random.fold_in(stream_key, 6), dim), (parts,), jnp.float32, smallest / len(shards), largest / len(shards))
        return jnp.repeat(jnp.exp(draws), shape[dim] // parts).reshape((-1,) + (1,) * (len(shape) - dim - 1))

    level = one(*shards[0])
    for cut in shards[1:]:
        level = level * one(*cut)
    return level


def gaussian(stream_key, extent, spread, reach, cuts=(), dtype=jnp.bfloat16):
    entries = jax.random.normal(stream_key, extent, jnp.float32) * spread
    if len(cuts) > 0:
        entries = steps_of(stream_key, extent, cuts, -0.22, 0.18) * entries
    return jnp.clip(entries, min=-reach, max=reach).astype(dtype)


def setup_inputs(seed: int = 0) -> dict:
    key_list = jax.random.split(jax.random.key(seed), 5)
    return {
        "activations": gaussian(key_list[0], (TOK, IN), 1.0, 6.0, ((0, 32), (1, 16))),
        "act_basis": gaussian(key_list[1], (IN, IN), IN ** -0.5, 0.03125, ((0, 16), (1, 32))),
        "out_grads": gaussian(key_list[2], (TOK, OUT), SEQ_LEN ** -0.5, 0.375, ((0, 16), (1, 32))),
        "grad_basis": gaussian(key_list[3], (OUT, OUT), OUT ** -0.5, 0.0625, ((0, 32), (1, 16))),
    }


def reference(activations, act_basis, out_grads, grad_basis):
    rotated_act = jnp.dot(activations, act_basis, preferred_element_type=jnp.float32).astype(jnp.bfloat16)
    rotated_grad = jnp.dot(out_grads, grad_basis, preferred_element_type=jnp.float32).astype(jnp.bfloat16)
    act_seq = rotated_act.astype(jnp.float32).reshape(SEQS, SEQ_LEN, IN)
    grad_seq = rotated_grad.astype(jnp.float32).reshape(SEQS, SEQ_LEN, OUT)
    if OUT % 512 == 0:
        block_rows = 512
    else:
        block_rows = OUT
    blocks = OUT // block_rows
    grad_blocks = jnp.moveaxis(grad_seq.reshape(SEQS, SEQ_LEN, blocks, block_rows), 2, 0)

    def one_block(grad_block):
        seq_grad = jnp.einsum("slo,sli->soi", grad_block, act_seq)
        return (jnp.sum(seq_grad * seq_grad, axis=0) / SEQS).astype(jnp.bfloat16)

    result = lax.map(one_block, grad_blocks)
    return result.reshape(OUT, IN)
```

```python
import functools

import jax
import jax.numpy as jnp
from jax import lax
from jax.experimental import pallas as pl
from jax.experimental.pallas import tpu as pltpu
from jax.sharding import PartitionSpec as P

MESH = pl.DeviceIdType.MESH
BF = jnp.bfloat16
F32 = jnp.float32


def flip(v, k):
    if k == 0:
        return v
    if k == 1:
        return v + 1 - 2 * (v % 2)
    if k == 2:
        return (v + 2) % 4
    return 3 - v


class Slots:
    def __init__(self):
        self.n = 0

    def take(self, k):
        first = self.n
        self.n += k
        return first


SLOTS = Slots()
ZA = SLOTS.take(4)
XP = SLOTS.take(4)
XM = SLOTS.take(4)
FP = SLOTS.take(4)
FM = SLOTS.take(4)
CA = SLOTS.take(16)
YR = SLOTS.take(4)
ZR = SLOTS.take(4)
ZG = SLOTS.take(4)
YP = SLOTS.take(4)
YM = SLOTS.take(4)
HP = SLOTS.take(4)
HM = SLOTS.take(4)
GZ = SLOTS.take(4)
GY = SLOTS.take(4)
QC = SLOTS.take(1)
QX = SLOTS.take(4)
QZ = SLOTS.take(4)
FZ = SLOTS.take(4)
FX = SLOTS.take(4)
FC = SLOTS.take(1)


def rows(start, size):
    return pl.ds(pl.multiple_of(start, size), size)


def kernel(
    act, basis, og, gbasis, out,
    a, w, own, part, r1, s1, s1b, r2, g,
    ogv, gb, q, qb, rc, q1, q1b, rx, q2, q2b, rz, fg, fgt, o,
    lsem, ssem, rsem,
):
    r, c = lax.axis_index("row"), lax.axis_index("col")
    y, zh = r // 4, r % 4
    zl, x, core = c // 8, (c // 2) % 4, c % 2
    half = a.shape[1] // 2

    def at(yy=y, zz=zh, ll=zl, xx=x, cc=core):
        return (yy * 4 + zz, ll * 8 + xx * 2 + cc)

    xp, xm = (x + 1) % 4, (x + 3) % 4
    yp, ym = (y + 1) % 4, (y + 3) % 4
    mate = 1 - core

    pending = []

    def copy(src, dst, slot, dev):
        return pltpu.make_async_remote_copy(
            src_ref=src,
            dst_ref=dst,
            send_sem=ssem.at[slot],
            recv_sem=rsem.at[slot],
            device_id=dev,
            device_id_type=MESH,
        )

    def send(src, dst, slot, dev):
        cp = copy(src, dst, slot, dev)
        cp.start()
        pending.append(cp)

    def arrived(dst, slot):
        copy(dst, dst, slot, at(cc=mate)).wait_recv()

    load_act = pltpu.make_async_copy(act, a.at[rows(16 * c, 16)], lsem.at[0])
    load_og = pltpu.make_async_copy(og, ogv.at[rows(32 * r, 32)], lsem.at[1])
    load_w = pltpu.make_async_copy(basis, w, lsem.at[2])
    load_gb = pltpu.make_async_copy(gbasis, gb, lsem.at[3])
    load_act.start()
    load_og.start()
    load_gb.start()
    load_w.start()

    barrier = pltpu.get_barrier_semaphore()
    partners = [at(cc=mate)]
    for k in (1, 2, 3):
        partners += [at(ll=flip(zl, k)), at(xx=flip(x, k)), at(yy=flip(y, k)), at(zz=flip(zh, k))]
    for dev in partners:
        pl.semaphore_signal(barrier, inc=1, device_id=dev, device_id_type=MESH)
    pl.semaphore_wait(barrier, len(partners))

    def piece(j, xx, cc):
        return rows(128 * flip(zl, j) + 32 * xx + 16 * cc, 16)

    def xsend(j):
        p = a.at[piece(j, x, core)]
        send(p, p, XP + j, at(xx=xp))
        send(p, p, XM + j, at(xx=xm))

    def csend(j, i):
        p = a.at[piece(j, (x, xm, xp, (x + 2) % 4)[i], core)]
        send(p, p, CA + 4 * j + i, at(cc=mate))

    def zrecv(j):
        arrived(a.at[piece(j, x, core)], ZA + j)
        xsend(j)
        csend(j, 0)

    def xforward(j):
        p = piece(j, xm, core)
        arrived(a.at[p], XP + j)
        h = a.at[p, pl.ds(0, half)]
        send(h, h, FP + j, at(xx=xp))
        csend(j, 1)
        p = piece(j, xp, core)
        arrived(a.at[p], XM + j)
        h = a.at[p, pl.ds(half, half)]
        send(h, h, FM + j, at(xx=xm))
        csend(j, 2)

    def xfinish(j):
        p = piece(j, (x + 2) % 4, core)
        arrived(a.at[p, pl.ds(0, half)], FP + j)
        arrived(a.at[p, pl.ds(half, half)], FM + j)
        csend(j, 3)

    def multiply(j):
        for i in range(4):
            arrived(a.at[piece(j, (x, xm, xp, (x + 2) % 4)[i], mate)], CA + 4 * j + i)
        b = flip(zl, j)
        block = rows(128 * b, 128)
        acc = jnp.dot(a[block, :], w[...], preferred_element_type=F32)
        m = (b - y + 4) % 4

        @pl.when(m == 0)
        def _():
            own[...] = acc

        @pl.when(m != 0)
        def _():
            part[block, :] = acc.astype(BF)
            copy(part.at[block], r1.at[m - 1], YR + m, at(yy=b)).start()

    load_act.wait()
    p = a.at[rows(16 * c, 16)]
    for k in (1, 2, 3):
        send(p, p, ZA + k, at(ll=flip(zl, k)))
    xsend(0)
    csend(0, 0)
    load_og.wait()
    p = ogv.at[rows(32 * r, 32)]
    for k in (1, 2, 3):
        send(p, p, GZ + k, at(zz=flip(zh, k)))

    xforward(0)
    zrecv(1)
    zrecv(2)
    xforward(1)
    xfinish(0)
    zrecv(3)
    xforward(2)
    load_w.wait()
    multiply(0)
    xfinish(1)
    xforward(3)
    for k in (1, 2, 3):
        arrived(ogv.at[rows(32 * (4 * y + flip(zh, k)), 32)], GZ + k)
    p = ogv.at[rows(128 * y, 128)]
    for k in (1, 2, 3):
        send(p, p, GY + k, at(yy=flip(y, k)))
    multiply(1)
    xfinish(2)
    multiply(2)
    xfinish(3)
    multiply(3)

    for k in (1, 2, 3):
        arrived(ogv.at[rows(128 * flip(y, k), 128)], GY + k)
    load_gb.wait()
    qv = jnp.dot(ogv[...], gb[...], preferred_element_type=F32).reshape(q.shape)
    q[...] = qv
    qb[...] = qv.astype(BF)
    send(qb.at[:, mate], rc, QC, at(cc=mate))

    total = own[...]
    for m in (1, 2, 3):
        arrived(r1.at[m - 1], YR + m)
        total = total + r1[m - 1].astype(F32)
    s1[...] = total
    s1b[...] = total.astype(BF)
    for k in (1, 2, 3):
        send(s1b.at[rows(32 * flip(zh, k), 32)], r2.at[k - 1], ZR + k, at(zz=flip(zh, k)))

    arrived(rc, QC)
    v = (q[:, core] + rc[...].astype(F32)).reshape(q1.shape)
    q1[...] = v
    q1b[...] = v.astype(BF)
    for k in (1, 2, 3):
        send(q1b.at[:, flip(x, k)], rx.at[k - 1], QX + k, at(xx=flip(x, k)))
    v = q1[:, x]
    for k in (1, 2, 3):
        arrived(rx.at[k - 1], QX + k)
        v = v + rx[k - 1].astype(F32)
    q2[...] = v
    q2b[...] = v.astype(BF)
    for k in (1, 2, 3):
        send(q2b.at[flip(zl, k)], rz.at[k - 1], QZ + k, at(ll=flip(zl, k)))
    v = q2[zl]
    for k in (1, 2, 3):
        arrived(rz.at[k - 1], QZ + k)
        v = v + rz[k - 1].astype(F32)
    fg[zl, x, core] = v.astype(BF)
    for k in (1, 2, 3):
        p = fg.at[zl, x, core]
        send(p, p, FZ + k, at(ll=flip(zl, k)))

    total = s1[rows(32 * zh, 32), :]
    for k in (1, 2, 3):
        arrived(r2.at[k - 1], ZR + k)
        total = total + r2[k - 1].astype(F32)
    g[rows(32 * r, 32), :] = total.astype(BF)

    def gpiece(j, yy):
        return rows(32 * (4 * yy + flip(zh, j)), 32)

    def gupper(j, yy):
        return rows(32 * (4 * yy + flip(zh, j)), 16)

    def glower(j, yy):
        return rows(32 * (4 * yy + flip(zh, j)) + 16, 16)

    def ysend(j):
        p = g.at[gpiece(j, y)]
        send(p, p, YP + j, at(yy=yp))
        send(p, p, YM + j, at(yy=ym))

    def yforward(j):
        arrived(g.at[gpiece(j, ym)], YP + j)
        p = g.at[gupper(j, ym)]
        send(p, p, HP + j, at(yy=yp))
        arrived(g.at[gpiece(j, yp)], YM + j)
        p = g.at[glower(j, yp)]
        send(p, p, HM + j, at(yy=ym))

    p = g.at[gpiece(0, y)]
    for k in (1, 2, 3):
        send(p, p, ZG + k, at(zz=flip(zh, k)))
    ysend(0)

    for k in (1, 2, 3):
        arrived(fg.at[flip(zl, k), x, core], FZ + k)
    p = fg.at[:, x, core]
    for k in (1, 2, 3):
        send(p, p, FX + k, at(xx=flip(x, k)))
    yforward(0)
    for k in (1, 2, 3):
        arrived(fg.at[:, flip(x, k), core], FX + k)
    p = fg.at[:, :, core]
    send(p, p, FC, at(cc=mate))
    arrived(fg.at[:, :, mate], FC)
    fgt[...] = fg[...].reshape(fgt.shape[1], fgt.shape[0]).T

    for j in (1, 2, 3):
        arrived(g.at[gpiece(j, y)], ZG + j)
        ysend(j)
    for j in (1, 2, 3):
        yforward(j)
    for j in range(4):
        arrived(g.at[gupper(j, (y + 2) % 4)], HP + j)
        arrived(g.at[glower(j, (y + 2) % 4)], HM + j)

    stores = []
    for i in range(4):
        block = pl.ds(128 * i, 128)
        s = jnp.dot(fgt[block, 0:256], g[0:256, :], preferred_element_type=F32)
        t = jnp.dot(fgt[block, 256:512], g[256:512, :], preferred_element_type=F32)
        o[block, :] = ((s * s + t * t) * 0.5).astype(BF)
        cp = pltpu.make_async_copy(o.at[block], out.at[block], lsem.at[4 + i])
        cp.start()
        stores.append(cp)

    for cp in pending:
        cp.wait_send()
    for m in (1, 2, 3):
        copy(part.at[pl.ds(0, 128)], r1.at[m - 1], YR + m, at(cc=mate)).wait_send()
    for cp in stores:
        cp.wait()


def solution(mesh):
    def local(activations, act_basis, out_grads, grad_basis):
        nin, nout = act_basis.shape[1], grad_basis.shape[1]
        tok = 512
        any_ = pl.BlockSpec(memory_space=pl.ANY)
        v = pltpu.VMEM
        return pl.pallas_call(
            kernel,
            out_shape=jax.ShapeDtypeStruct((nout, nin), BF),
            in_specs=[any_] * 4,
            out_specs=any_,
            scratch_shapes=[
                v((tok, act_basis.shape[0]), BF),
                v(act_basis.shape, BF),
                v((128, nin), F32),
                v((tok, nin), BF),
                v((3, 128, nin), BF),
                v((128, nin), F32),
                v((128, nin), BF),
                v((3, 32, nin), BF),
                v((tok, nin), BF),
                v((tok, out_grads.shape[1]), BF),
                v(grad_basis.shape, BF),
                v((16, 2, 16, nout), F32),
                v((16, 2, 16, nout), BF),
                v((16, 16, nout), BF),
                v((4, 4, 16, nout), F32),
                v((4, 4, 16, nout), BF),
                v((3, 4, 16, nout), BF),
                v((4, 16, nout), F32),
                v((4, 16, nout), BF),
                v((3, 16, nout), BF),
                v((4, 4, 2, 16, nout), BF),
                v((nout, tok), BF),
                v((nout, nin), BF),
                pltpu.SemaphoreType.DMA((8,)),
                pltpu.SemaphoreType.DMA((SLOTS.n,)),
                pltpu.SemaphoreType.DMA((SLOTS.n,)),
            ],
            compiler_params=pltpu.CompilerParams(
                collective_id=0, has_side_effects=True, vmem_limit_bytes=48 * 1024 * 1024
            ),
        )(activations, act_basis, out_grads, grad_basis)

    return jax.shard_map(
        local,
        mesh=mesh,
        in_specs=(P("col", "row"), P("row", "col"), P("row", "col"), P("col", "row")),
        out_specs=P("row", "col"),
        check_vma=False,
    )
```

```python
import jax
import jax.numpy as jnp
from jax import lax
from jax.experimental import pallas as pl
from jax.experimental.pallas import tpu as pltpu
from jax.sharding import PartitionSpec as P

MESH = pl.DeviceIdType.MESH
BF = jnp.bfloat16
F32 = jnp.float32


def flip(v, k):
    if k == 0:
        return v
    if k == 1:
        return v + 1 - 2 * (v % 2)
    if k == 2:
        return (v + 2) % 4
    return 3 - v


class Slots:
    def __init__(self):
        self.n = 0

    def take(self, k):
        first = self.n
        self.n += k
        return first


SLOTS = Slots()
ZA = SLOTS.take(4)
XP = SLOTS.take(4)
XM = SLOTS.take(4)
FP = SLOTS.take(4)
FM = SLOTS.take(4)
CA = SLOTS.take(16)
YS = SLOTS.take(6)
ZS = SLOTS.take(6)
ZG = SLOTS.take(4)
YP = SLOTS.take(4)
YM = SLOTS.take(4)
HP = SLOTS.take(4)
HM = SLOTS.take(4)
GZ = SLOTS.take(4)
GY = SLOTS.take(4)
QC = SLOTS.take(1)
QX = SLOTS.take(4)
QZ = SLOTS.take(4)
FZ = SLOTS.take(4)
FX = SLOTS.take(4)
FC = SLOTS.take(1)
LEFT, RIGHT = pl.ds(0, 512), pl.ds(512, 384)


def rows(start, size):
    return pl.ds(pl.multiple_of(start, size), size)


def kernel(
    act, basis, og, gbasis, out,
    a, w, own, part, yl, yr, ysl, ysr, r1, s1, s1b, zbl, zbr, zsl, zsr, r2, g,
    ogv, gb, q, rc, q1, q1b, rx, q2, rz, fg, fgt, sq,
    lsem, ssem, rsem,
):
    r, c = lax.axis_index("row"), lax.axis_index("col")
    y, zh = r // 4, r % 4
    zl, x, core = c // 8, (c // 2) % 4, c % 2
    half = a.shape[1] // 2

    def at(yy=y, zz=zh, ll=zl, xx=x, cc=core):
        return (yy * 4 + zz, ll * 8 + xx * 2 + cc)

    xp, xm = (x + 1) % 4, (x + 3) % 4
    yp, ym = (y + 1) % 4, (y + 3) % 4
    zp, zm = (zh + 1) % 4, (zh + 3) % 4
    mate = 1 - core

    pending = []

    def copy(src, dst, slot, dev):
        return pltpu.make_async_remote_copy(
            src_ref=src,
            dst_ref=dst,
            send_sem=ssem.at[slot],
            recv_sem=rsem.at[slot],
            device_id=dev,
            device_id_type=MESH,
        )

    def send(src, dst, slot, dev):
        cp = copy(src, dst, slot, dev)
        cp.start()
        pending.append(cp)

    def arrived(dst, slot):
        copy(dst, dst, slot, at(cc=mate)).wait_recv()

    load_act = pltpu.make_async_copy(act, a.at[rows(16 * c, 16)], lsem.at[0])
    load_og = pltpu.make_async_copy(og, ogv.at[rows(32 * r, 32)], lsem.at[1])
    load_w = pltpu.make_async_copy(basis, w, lsem.at[2])
    load_gb = pltpu.make_async_copy(gbasis, gb, lsem.at[3])
    load_act.start()
    load_og.start()
    load_gb.start()
    load_w.start()

    barrier = pltpu.get_barrier_semaphore()
    partners = [at(cc=mate)]
    for k in (1, 2, 3):
        partners += [at(ll=flip(zl, k)), at(xx=flip(x, k)), at(yy=flip(y, k))]
    partners += [at(zz=zp), at(zz=zm)]
    for dev in partners:
        pl.semaphore_signal(barrier, inc=1, device_id=dev, device_id_type=MESH)
    pl.semaphore_wait(barrier, len(partners))

    def piece(j, xx, cc):
        return rows(128 * flip(zl, j) + 32 * xx + 16 * cc, 16)

    near = (x, xm, xp, (x + 2) % 4)

    def xsend(j):
        p = a.at[piece(j, x, core)]
        send(p, p, XP + j, at(xx=xp))
        send(p, p, XM + j, at(xx=xm))

    def csend(j, i):
        p = a.at[piece(j, near[i], core)]
        send(p, p, CA + 4 * j + i, at(cc=mate))

    def zrecv(j):
        arrived(a.at[piece(j, x, core)], ZA + j)
        xsend(j)
        csend(j, 0)

    def xforward(j):
        p = piece(j, xm, core)
        arrived(a.at[p], XP + j)
        h = a.at[p, pl.ds(0, half)]
        send(h, h, FP + j, at(xx=xp))
        csend(j, 1)
        p = piece(j, xp, core)
        arrived(a.at[p], XM + j)
        h = a.at[p, pl.ds(half, half)]
        send(h, h, FM + j, at(xx=xm))
        csend(j, 2)

    def xfinish(j):
        p = piece(j, near[3], core)
        arrived(a.at[p, pl.ds(0, half)], FP + j)
        arrived(a.at[p, pl.ds(half, half)], FM + j)
        csend(j, 3)

    def block_of(j):
        b = flip(zl, j)
        return rows(128 * b, 128), (b - y + 4) % 4

    def ycopy(i, block):
        src, dst, dev = (
            (part.at[block, LEFT], yl, ym),
            (part.at[block, RIGHT], yr, yp),
            (part.at[block, LEFT], r1.at[1, :, LEFT], yp),
            (ysr, r1.at[1, :, RIGHT], yp),
            (part.at[block, RIGHT], r1.at[0, :, RIGHT], ym),
            (ysl, r1.at[0, :, LEFT], ym),
        )[i]
        return copy(src, dst, YS + i, at(yy=dev))

    def multiply(j):
        for i in range(4):
            arrived(a.at[piece(j, near[i], mate)], CA + 4 * j + i)
        block, m = block_of(j)
        acc = jnp.dot(a[block, :], w[...], preferred_element_type=F32)
        own[block, :] = acc
        part[block, :] = acc.astype(BF)

        @pl.when(m == 2)
        def _():
            ycopy(0, block).start()
            ycopy(1, block).start()

        @pl.when(m == 1)
        def _():
            ycopy(2, block).start()

        @pl.when(m == 3)
        def _():
            ycopy(4, block).start()

    def addsend(j):
        block, m = block_of(j)

        @pl.when(m == 1)
        def _():
            arrived(yr, YS + 1)
            ysr[...] = (own[block, RIGHT] + yr[...].astype(F32)).astype(BF)
            ycopy(3, block).start()

        @pl.when(m == 3)
        def _():
            arrived(yl, YS + 0)
            ysl[...] = (own[block, LEFT] + yl[...].astype(F32)).astype(BF)
            ycopy(5, block).start()

    zring = (zh, zm, zp, (zh + 2) % 4)

    def gz(i, upper=None):
        first = 128 * y + 32 * zring[i]
        if upper is None:
            return ogv.at[rows(first, 32)]
        return ogv.at[rows(first + 16 * upper, 16)]

    load_act.wait()
    p = a.at[rows(16 * c, 16)]
    for k in (1, 2, 3):
        send(p, p, ZA + k, at(ll=flip(zl, k)))
    xsend(0)
    csend(0, 0)
    load_og.wait()
    send(gz(0), gz(0), GZ + 0, at(zz=zp))
    send(gz(0), gz(0), GZ + 1, at(zz=zm))

    zrecv(1)
    xforward(0)
    zrecv(2)
    zrecv(3)
    xforward(1)
    xfinish(0)
    arrived(gz(1), GZ + 0)
    send(gz(1, 0), gz(1, 0), GZ + 2, at(zz=zp))
    arrived(gz(2), GZ + 1)
    send(gz(2, 1), gz(2, 1), GZ + 3, at(zz=zm))
    xforward(2)
    xfinish(1)
    load_w.wait()
    multiply(0)
    xforward(3)
    xfinish(2)
    multiply(1)
    addsend(0)
    xfinish(3)
    arrived(gz(3, 0), GZ + 2)
    arrived(gz(3, 1), GZ + 3)
    p = ogv.at[rows(128 * y, 128)]
    for k in (1, 2, 3):
        send(p, p, GY + k, at(yy=flip(y, k)))
    multiply(2)
    addsend(1)
    multiply(3)
    addsend(2)
    addsend(3)

    for k in (1, 2, 3):
        arrived(ogv.at[rows(128 * flip(y, k), 128)], GY + k)
    load_gb.wait()
    q[...] = jnp.dot(ogv[...], gb[...], preferred_element_type=F32).reshape(q.shape)
    send(q.at[:, mate], rc, QC, at(cc=mate))

    arrived(r1.at[1, :, LEFT], YS + 2)
    arrived(r1.at[0, :, RIGHT], YS + 4)
    arrived(r1.at[1, :, RIGHT], YS + 3)
    arrived(r1.at[0, :, LEFT], YS + 5)
    total = own[rows(128 * y, 128), :] + r1[0].astype(F32) + r1[1].astype(F32)
    s1[...] = total
    s1b[...] = total.astype(BF)

    def to(i):
        return rows(32 * zring[i], 32)

    send(s1b.at[to(3), LEFT], zbl, ZS + 0, at(zz=zm))
    send(s1b.at[to(3), RIGHT], zbr, ZS + 1, at(zz=zp))
    send(s1b.at[to(2), LEFT], r2.at[1, :, LEFT], ZS + 2, at(zz=zp))
    send(s1b.at[to(1), RIGHT], r2.at[0, :, RIGHT], ZS + 4, at(zz=zm))

    arrived(rc, QC)
    v = (q[:, core] + rc[...]).reshape(q1.shape)
    q1[...] = v
    q1b[...] = v.astype(BF)
    for k in (1, 2, 3):
        send(q1b.at[:, flip(x, k)], rx.at[k - 1], QX + k, at(xx=flip(x, k)))

    arrived(zbr, ZS + 1)
    zsr[...] = (s1[to(2), RIGHT] + zbr[...].astype(F32)).astype(BF)
    send(zsr, r2.at[1, :, RIGHT], ZS + 3, at(zz=zp))
    arrived(zbl, ZS + 0)
    zsl[...] = (s1[to(1), LEFT] + zbl[...].astype(F32)).astype(BF)
    send(zsl, r2.at[0, :, LEFT], ZS + 5, at(zz=zm))

    v = q1[:, x]
    for k in (1, 2, 3):
        arrived(rx.at[k - 1], QX + k)
        v = v + rx[k - 1].astype(F32)
    q2[...] = v
    for k in (1, 2, 3):
        send(q2.at[flip(zl, k)], rz.at[k - 1], QZ + k, at(ll=flip(zl, k)))

    arrived(r2.at[1, :, LEFT], ZS + 2)
    arrived(r2.at[0, :, RIGHT], ZS + 4)
    arrived(r2.at[1, :, RIGHT], ZS + 3)
    arrived(r2.at[0, :, LEFT], ZS + 5)
    total = s1[to(0), :] + r2[0].astype(F32) + r2[1].astype(F32)
    g[rows(32 * r, 32), :] = total.astype(BF)

    def gpiece(i, yy):
        return rows(32 * (4 * yy + zring[i]), 32)

    def ysend(i):
        p = g.at[gpiece(i, y)]
        send(p, p, YP + i, at(yy=yp))
        send(p, p, YM + i, at(yy=ym))

    def yforward(i):
        p = gpiece(i, ym)
        arrived(g.at[p], YP + i)
        h = g.at[p, LEFT]
        send(h, h, HP + i, at(yy=yp))
        p = gpiece(i, yp)
        arrived(g.at[p], YM + i)
        h = g.at[p, RIGHT]
        send(h, h, HM + i, at(yy=ym))

    p = g.at[gpiece(0, y)]
    send(p, p, ZG + 0, at(zz=zp))
    send(p, p, ZG + 1, at(zz=zm))
    ysend(0)

    v = q2[zl]
    for k in (1, 2, 3):
        arrived(rz.at[k - 1], QZ + k)
        v = v + rz[k - 1]
    p = fg.at[zl, x, core]
    p[...] = v.astype(BF)
    for k in (1, 2, 3):
        send(p, p, FZ + k, at(ll=flip(zl, k)))

    p = gpiece(1, y)
    arrived(g.at[p], ZG + 0)
    h = g.at[p, LEFT]
    send(h, h, ZG + 2, at(zz=zp))
    ysend(1)
    p = gpiece(2, y)
    arrived(g.at[p], ZG + 1)
    h = g.at[p, RIGHT]
    send(h, h, ZG + 3, at(zz=zm))
    ysend(2)
    yforward(0)

    for k in (1, 2, 3):
        arrived(fg.at[flip(zl, k), x, core], FZ + k)
    p = fg.at[:, x, core]
    for k in (1, 2, 3):
        send(p, p, FX + k, at(xx=flip(x, k)))

    p = gpiece(3, y)
    arrived(g.at[p, LEFT], ZG + 2)
    arrived(g.at[p, RIGHT], ZG + 3)
    ysend(3)

    for k in (1, 2, 3):
        arrived(fg.at[:, flip(x, k), core], FX + k)
    p = fg.at[:, :, core]
    send(p, p, FC, at(cc=mate))
    for i in (1, 2, 3):
        yforward(i)
    arrived(fg.at[:, :, mate], FC)
    fgt[...] = fg[...].reshape(fgt.shape[1], fgt.shape[0]).T

    mine = 256 * (y // 2)
    other = 256 - mine
    cuts = [pl.ds(256 * i, min(256, g.shape[1] - 256 * i)) for i in range(4)]
    for cut in cuts:
        s = jnp.dot(fgt[:, rows(mine, 256)], g[rows(mine, 256), cut], preferred_element_type=F32)
        sq[:, cut] = s * s
    for i in range(4):
        p = gpiece(i, (y + 2) % 4)
        arrived(g.at[p, LEFT], HP + i)
        arrived(g.at[p, RIGHT], HM + i)
    for cut in cuts:
        s = jnp.dot(fgt[:, rows(other, 256)], g[rows(other, 256), cut], preferred_element_type=F32)
        out[:, cut] = ((sq[:, cut] + s * s) * 0.5).astype(BF)

    for cp in pending:
        cp.wait_send()
    for i in range(6):
        ycopy(i, pl.ds(0, 128)).wait_send()


def solution(mesh):
    def local(activations, act_basis, out_grads, grad_basis):
        nin, nout = act_basis.shape[1], grad_basis.shape[1]
        tok = 512
        any_ = pl.BlockSpec(memory_space=pl.ANY)
        v = pltpu.VMEM
        return pl.pallas_call(
            kernel,
            out_shape=pltpu.VMEM((nout, nin), BF),
            in_specs=[any_] * 4,
            out_specs=pl.BlockSpec(memory_space=pltpu.VMEM),
            scratch_shapes=[
                v((tok, act_basis.shape[0]), BF),
                v(act_basis.shape, BF),
                v((tok, nin), F32),
                v((tok, nin), BF),
                v((128, 512), BF),
                v((128, 384), BF),
                v((128, 512), BF),
                v((128, 384), BF),
                v((2, 128, nin), BF),
                v((128, nin), F32),
                v((128, nin), BF),
                v((32, 512), BF),
                v((32, 384), BF),
                v((32, 512), BF),
                v((32, 384), BF),
                v((2, 32, nin), BF),
                v((tok, nin), BF),
                v((tok, out_grads.shape[1]), BF),
                v(grad_basis.shape, BF),
                v((16, 2, 16, nout), F32),
                v((16, 16, nout), F32),
                v((4, 4, 16, nout), F32),
                v((4, 4, 16, nout), BF),
                v((3, 4, 16, nout), BF),
                v((4, 16, nout), F32),
                v((3, 16, nout), F32),
                v((4, 4, 2, 16, nout), BF),
                v((nout, tok), BF),
                v((nout, nin), F32),
                pltpu.SemaphoreType.DMA((4,)),
                pltpu.SemaphoreType.DMA((SLOTS.n,)),
                pltpu.SemaphoreType.DMA((SLOTS.n,)),
            ],
            compiler_params=pltpu.CompilerParams(
                collective_id=0, has_side_effects=True
            ),
        )(activations, act_basis, out_grads, grad_basis)

    return jax.shard_map(
        local,
        mesh=mesh,
        in_specs=(P("col", "row"), P("row", "col"), P("row", "col"), P("col", "row")),
        out_specs=P("row", "col"),
        check_vma=False,
    )
```

```python
import jax
import jax.numpy as jnp
from jax import lax
from jax.experimental import pallas as pl
from jax.experimental.pallas import tpu as pltpu
from jax.sharding import PartitionSpec as P

MESH = pl.DeviceIdType.MESH
BF = jnp.bfloat16
F32 = jnp.float32


def flip(v, k):
    if k == 0:
        return v
    if k == 1:
        return v + 1 - 2 * (v % 2)
    if k == 2:
        return (v + 2) % 4
    return 3 - v


class Slots:
    def __init__(self):
        self.n = 0

    def take(self, k):
        first = self.n
        self.n += k
        return first


SLOTS = Slots()
ZA = SLOTS.take(4)
XP = SLOTS.take(4)
XM = SLOTS.take(4)
XF = SLOTS.take(4)
CA = SLOTS.take(4)
YH = SLOTS.take(4)
YR = SLOTS.take(4)
ZB = SLOTS.take(2)
ZR = SLOTS.take(1)
ZG = SLOTS.take(5)
YG = SLOTS.take(4)
YF = SLOTS.take(2)
GZ = SLOTS.take(2)
GY = SLOTS.take(3)
GF = SLOTS.take(1)
QC = SLOTS.take(1)
QX = SLOTS.take(1)
QZ = SLOTS.take(1)
FZ = SLOTS.take(1)
FX = SLOTS.take(1)
FC = SLOTS.take(1)
LEFT, RIGHT = pl.ds(0, 512), pl.ds(512, 384)


def rows(start, size):
    return pl.ds(pl.multiple_of(start, size), size)


def kernel(
    act, basis, og, gbasis, out,
    a, w, own, part, yl, yr, ysl, ysr, r1, s1, s1b, zbl, zbr, zsl, zsr, r2, g,
    ogv, gb, q, rc, q1, q1b, rx, q2, q2b, rz, fg, fgt, sq, sent,
    lsem, ssem, rsem,
):
    r, c = lax.axis_index("row"), lax.axis_index("col")
    y, zh = r // 4, r % 4
    zl, x, core = c // 8, (c // 2) % 4, c % 2
    half = a.shape[1] // 2

    def at(yy=y, zz=zh, ll=zl, xx=x, cc=core):
        return (yy * 4 + zz, ll * 8 + xx * 2 + cc)

    xp, xm = (x + 1) % 4, (x + 3) % 4
    yp, ym = (y + 1) % 4, (y + 3) % 4
    zp, zm = (zh + 1) % 4, (zh + 3) % 4
    mate = 1 - core

    def copy(src, dst, slot, dev):
        return pltpu.make_async_remote_copy(
            src_ref=src,
            dst_ref=dst,
            send_sem=ssem.at[0],
            recv_sem=rsem.at[slot],
            device_id=dev,
            device_id_type=MESH,
        )

    def send(src, dst, slot, dev):
        copy(src, dst, slot, dev).start()

    def arrived(like, slot):
        copy(like, like, slot, at(cc=mate)).wait_recv()

    load_act = pltpu.make_async_copy(act, a.at[rows(16 * c, 16)], lsem.at[0])
    load_og = pltpu.make_async_copy(og, ogv.at[rows(32 * r, 32)], lsem.at[1])
    load_w = pltpu.make_async_copy(basis, w, lsem.at[2])
    load_gb = pltpu.make_async_copy(gbasis, gb, lsem.at[3])
    load_act.start()
    load_og.start()
    load_gb.start()
    load_w.start()

    barrier = pltpu.get_barrier_semaphore()
    partners = [at(cc=mate)]
    for k in (1, 2, 3):
        partners += [at(ll=flip(zl, k)), at(xx=flip(x, k)), at(yy=flip(y, k))]
    partners += [at(zz=zp), at(zz=zm)]
    for dev in partners:
        pl.semaphore_signal(barrier, inc=1, device_id=dev, device_id_type=MESH)
    pl.semaphore_wait(barrier, len(partners))

    def piece(j, xx, cc):
        return rows(128 * flip(zl, j) + 32 * xx + 16 * cc, 16)

    near = (x, xm, xp, (x + 2) % 4)

    def xsend(j):
        p = a.at[piece(j, x, core)]
        send(p, p, XP + j, at(xx=xp))
        send(p, p, XM + j, at(xx=xm))

    def csend(j, i):
        p = a.at[piece(j, near[i], core)]
        send(p, p, CA + j, at(cc=mate))

    def zrecv(j):
        arrived(a.at[piece(j, x, core)], ZA + j)
        xsend(j)
        csend(j, 0)

    def xforward(j):
        p = piece(j, xm, core)
        arrived(a.at[p], XP + j)
        h = a.at[p, pl.ds(0, half)]
        send(h, h, XF + j, at(xx=xp))
        csend(j, 1)
        p = piece(j, xp, core)
        arrived(a.at[p], XM + j)
        h = a.at[p, pl.ds(half, half)]
        send(h, h, XF + j, at(xx=xm))
        csend(j, 2)

    def xfinish(j):
        arrived(a.at[piece(j, near[3], core)], XF + j)
        csend(j, 3)

    def sub(j, yy):
        return rows(128 * flip(zl, j) + 32 * yy, 32)

    def multiply(j):
        arrived(a.at[pl.ds(0, 64)], CA + j)
        block = rows(128 * flip(zl, j), 128)
        acc = jnp.dot(a[block, :], w[...], preferred_element_type=F32)
        own[block, :] = acc
        part[block, :] = acc.astype(BF)
        far = sub(j, (y + 2) % 4)
        send(part.at[far, LEFT], yl.at[j], YH + j, at(yy=ym))
        send(part.at[far, RIGHT], yr.at[j], YH + j, at(yy=yp))
        send(part.at[sub(j, yp), LEFT], r1.at[j, 1, :, LEFT], YR + j, at(yy=yp))
        send(part.at[sub(j, ym), RIGHT], r1.at[j, 0, :, RIGHT], YR + j, at(yy=ym))

    def addsend(j):
        arrived(r1.at[j, 0], YH + j)
        ysr[j] = (own[sub(j, yp), RIGHT] + yr[j].astype(F32)).astype(BF)
        send(ysr.at[j], r1.at[j, 1, :, RIGHT], YR + j, at(yy=yp))
        ysl[j] = (own[sub(j, ym), LEFT] + yl[j].astype(F32)).astype(BF)
        send(ysl.at[j], r1.at[j, 0, :, LEFT], YR + j, at(yy=ym))

    def owner(j):
        return (flip(zl, j) - zh + 4) % 4

    def ysum(j):
        arrived(r1.at[j], YR + j)
        total = own[sub(j, y), :] + r1[j, 0].astype(F32) + r1[j, 1].astype(F32)
        s1[j] = total
        s1b[j] = total.astype(BF)
        m = owner(j)

        @pl.when(m == 2)
        def _():
            send(s1b.at[j, :, LEFT], zbl, ZB + 0, at(zz=zm))
            send(s1b.at[j, :, RIGHT], zbr, ZB + 1, at(zz=zp))

        @pl.when(m == 1)
        def _():
            send(s1b.at[j, :, LEFT], r2.at[1, :, LEFT], ZR, at(zz=zp))

        @pl.when(m == 3)
        def _():
            send(s1b.at[j, :, RIGHT], r2.at[0, :, RIGHT], ZR, at(zz=zm))

    def zadd(j):
        m = owner(j)

        @pl.when(m == 1)
        def _():
            arrived(zbr, ZB + 1)
            zsr[...] = (s1[j, :, RIGHT] + zbr[...].astype(F32)).astype(BF)
            send(zsr, r2.at[1, :, RIGHT], ZR, at(zz=zp))

        @pl.when(m == 3)
        def _():
            arrived(zbl, ZB + 0)
            zsl[...] = (s1[j, :, LEFT] + zbl[...].astype(F32)).astype(BF)
            send(zsl, r2.at[0, :, LEFT], ZR, at(zz=zm))

    def ysend(j):
        p = g.at[sub(j, y)]
        send(p, p, YG + j, at(yy=yp))
        send(p, p, YG + j, at(yy=ym))

    def yforward(j):
        arrived(g.at[pl.ds(0, 64)], YG + j)
        h = g.at[sub(j, ym), LEFT]
        send(h, h, YF + j // 2, at(yy=yp))
        h = g.at[sub(j, yp), RIGHT]
        send(h, h, YF + j // 2, at(yy=ym))

    def gsend(j, side, slot, dev):
        h = g.at[sub(j, y), side]
        send(h, h, ZG + slot, at(zz=dev))

    def round_own(j):
        @pl.when(owner(j) == 0)
        def _():
            arrived(r2, ZR)
            total = s1[j] + r2[0].astype(F32) + r2[1].astype(F32)
            g[sub(j, y), :] = total.astype(BF)
            gsend(j, LEFT, 0, zp)
            gsend(j, RIGHT, 1, zm)
            gsend(j, RIGHT, 2, zp)
            gsend(j, LEFT, 3, zm)
            ysend(j)

    def take_near(j):
        m = owner(j)

        @pl.when(m == 3)
        def _():
            arrived(g.at[sub(j, y), LEFT], ZG + 0)
            gsend(j, LEFT, 4, zp)
            arrived(g.at[sub(j, y), RIGHT], ZG + 2)
            ysend(j)

        @pl.when(m == 1)
        def _():
            arrived(g.at[sub(j, y), RIGHT], ZG + 1)
            gsend(j, RIGHT, 4, zm)
            arrived(g.at[sub(j, y), LEFT], ZG + 3)
            ysend(j)

    def take_far(j):
        @pl.when(owner(j) == 2)
        def _():
            arrived(g.at[sub(j, y)], ZG + 4)
            ysend(j)

    def forward_own(j):
        @pl.when(owner(j) == 0)
        def _():
            yforward(j)

    def forward_near(j):
        @pl.when(owner(j) % 2 == 1)
        def _():
            yforward(j)

    def forward_far(j):
        @pl.when(owner(j) == 2)
        def _():
            yforward(j)

    zring = (zh, zm, zp, (zh + 2) % 4)

    def gz(i, yy=y):
        return ogv.at[rows(128 * yy + 32 * zring[i], 32)]

    def gz_half(i, lower, yy=y):
        return ogv.at[rows(128 * yy + 32 * zring[i] + 16 * lower, 16)]

    def g_y(i, slot):
        send(gz(i), gz(i), GY + slot, at(yy=yp))
        send(gz(i), gz(i), GY + slot, at(yy=ym))

    def g_yforward(pieces, slot):
        arrived(ogv.at[pl.ds(0, 64 * len(pieces))], GY + slot)
        for i in pieces:
            h = gz_half(i, 0, ym)
            send(h, h, GF, at(yy=yp))
            h = gz_half(i, 1, yp)
            send(h, h, GF, at(yy=ym))

    def g_near():
        arrived(ogv.at[pl.ds(0, 64)], GZ + 0)
        h = gz_half(1, 0)
        send(h, h, GZ + 1, at(zz=zp))
        h = gz_half(2, 1)
        send(h, h, GZ + 1, at(zz=zm))
        g_y(1, 1)
        g_y(2, 1)

    def g_far():
        arrived(ogv.at[pl.ds(0, 32)], GZ + 1)
        g_y(3, 2)

    def q_core():
        arrived(ogv.at[pl.ds(0, 128)], GF)
        load_gb.wait()
        q[...] = jnp.dot(ogv[...], gb[...], preferred_element_type=F32).reshape(q.shape)
        send(q.at[:, mate], rc, QC, at(cc=mate))

    def q_x():
        arrived(rc, QC)
        v = (q[:, core] + rc[...]).reshape(q1.shape)
        q1[...] = v
        q1b[...] = v.astype(BF)
        for k in (1, 2, 3):
            send(q1b.at[:, flip(x, k)], rx.at[k - 1], QX, at(xx=flip(x, k)))

    def q_z():
        arrived(rx, QX)
        v = q1[:, x]
        for k in (1, 2, 3):
            v = v + rx[k - 1].astype(F32)
        q2[...] = v
        q2b[...] = v.astype(BF)
        for k in (1, 2, 3):
            send(q2b.at[flip(zl, k)], rz.at[k - 1], QZ, at(ll=flip(zl, k)))

    def f_z():
        arrived(rz, QZ)
        p = fg.at[zl, x, core]
        p[...] = (q2[zl] + rz[0].astype(F32) + rz[1].astype(F32) + rz[2].astype(F32)).astype(BF)
        for k in (1, 2, 3):
            send(p, p, FZ, at(ll=flip(zl, k)))

    def f_x():
        arrived(fg.at[0, pl.ds(0, 3), 0], FZ)
        p = fg.at[:, x, core]
        for k in (1, 2, 3):
            send(p, p, FX, at(xx=flip(x, k)))

    def f_core():
        arrived(fg.at[pl.ds(0, 3), :, 0], FX)
        p = fg.at[:, :, core]
        send(p, p, FC, at(cc=mate))

    def f_done():
        arrived(fg.at[:, :, mate], FC)
        fgt[...] = fg[...].reshape(fgt.shape[1], fgt.shape[0]).T

    load_act.wait()
    p = a.at[rows(16 * c, 16)]
    for k in (1, 2, 3):
        send(p, p, ZA + k, at(ll=flip(zl, k)))
    xsend(0)
    csend(0, 0)
    load_og.wait()
    send(gz(0), gz(0), GZ + 0, at(zz=zp))
    send(gz(0), gz(0), GZ + 0, at(zz=zm))

    g_y(0, 0)
    zrecv(1)
    xforward(0)
    zrecv(2)
    zrecv(3)
    xforward(1)
    xfinish(0)
    xforward(2)
    g_near()
    xfinish(1)
    g_yforward((0,), 0)
    xforward(3)
    load_w.wait()
    multiply(0)
    xfinish(2)
    multiply(1)
    addsend(0)
    xfinish(3)
    g_yforward((1, 2), 1)
    multiply(2)
    g_far()
    addsend(1)
    ysum(0)
    multiply(3)
    g_yforward((3,), 2)
    addsend(2)
    ysum(1)
    addsend(3)
    q_core()
    ysum(2)
    zadd(0)
    q_x()
    ysum(3)
    zadd(1)
    zadd(2)
    q_z()
    round_own(0)
    zadd(3)
    round_own(1)
    round_own(2)
    forward_own(0)
    f_z()
    round_own(3)
    forward_own(1)
    take_near(0)
    forward_own(2)
    take_near(1)
    forward_own(3)
    f_x()
    take_near(2)
    forward_near(0)
    take_near(3)
    forward_near(1)
    take_far(0)
    take_far(1)
    forward_near(2)
    f_core()
    take_far(2)
    forward_near(3)
    forward_far(0)
    take_far(3)
    forward_far(1)
    f_done()
    forward_far(2)
    forward_far(3)

    mine = 256 * (zl // 2)
    other = 256 - mine
    cuts = [pl.ds(256 * i, min(256, g.shape[1] - 256 * i)) for i in range(4)]
    arrived(g.at[pl.ds(0, 64)], YF + 0)
    for cut in cuts:
        s = jnp.dot(fgt[:, rows(mine, 256)], g[rows(mine, 256), cut], preferred_element_type=F32)
        sq[:, cut] = s * s
    arrived(g.at[pl.ds(0, 64)], YF + 1)
    for cut in cuts:
        s = jnp.dot(fgt[:, rows(other, 256)], g[rows(other, 256), cut], preferred_element_type=F32)
        out[:, cut] = ((sq[:, cut] + s * s) * 0.5).astype(BF)

    copy(sent, sent, 0, at(cc=mate)).wait_send()


def solution(mesh):
    def local(activations, act_basis, out_grads, grad_basis):
        nin, nout = act_basis.shape[1], grad_basis.shape[1]
        tok = 512
        apiece, gpiece = 2 * activations.size, 2 * 32 * nin
        opiece, fpiece = 2 * out_grads.size, 2 * 16 * nout
        sent = (
            (3 + 4 * 3 + 16) * apiece
            + (4 * 3 + 3 + 3 + 4 * 3) * gpiece
            + (3 + 3 * 4) * opiece
            + (2 * 16 + 3 * 4 + 3) * fpiece
            + (3 + 3 * 4 + 16) * fpiece
        )
        any_ = pl.BlockSpec(memory_space=pl.ANY)
        v = pltpu.VMEM
        return pl.pallas_call(
            kernel,
            out_shape=pltpu.VMEM((nout, nin), BF),
            in_specs=[any_] * 4,
            out_specs=pl.BlockSpec(memory_space=pltpu.VMEM),
            scratch_shapes=[
                v((tok, act_basis.shape[0]), BF),
                v(act_basis.shape, BF),
                v((tok, nin), F32),
                v((tok, nin), BF),
                v((4, 32, 512), BF),
                v((4, 32, 384), BF),
                v((4, 32, 512), BF),
                v((4, 32, 384), BF),
                v((4, 2, 32, nin), BF),
                v((4, 32, nin), F32),
                v((4, 32, nin), BF),
                v((32, 512), BF),
                v((32, 384), BF),
                v((32, 512), BF),
                v((32, 384), BF),
                v((2, 32, nin), BF),
                v((tok, nin), BF),
                v((tok, out_grads.shape[1]), BF),
                v(grad_basis.shape, BF),
                v((16, 2, 16, nout), F32),
                v((16, 16, nout), F32),
                v((4, 4, 16, nout), F32),
                v((4, 4, 16, nout), BF),
                v((3, 4, 16, nout), BF),
                v((4, 16, nout), F32),
                v((4, 16, nout), BF),
                v((3, 16, nout), BF),
                v((4, 4, 2, 16, nout), BF),
                v((nout, tok), BF),
                v((nout, nin), F32),
                v((sent // 256, 128), BF),
                pltpu.SemaphoreType.DMA((4,)),
                pltpu.SemaphoreType.DMA((1,)),
                pltpu.SemaphoreType.DMA((SLOTS.n,)),
            ],
            compiler_params=pltpu.CompilerParams(
                collective_id=0, has_side_effects=True
            ),
        )(activations, act_basis, out_grads, grad_basis)

    return jax.shard_map(
        local,
        mesh=mesh,
        in_specs=(P("col", "row"), P("row", "col"), P("row", "col"), P("col", "row")),
        out_specs=P("row", "col"),
        check_vma=False,
    )
```

```python
import jax
import jax.numpy as jnp
from jax import lax
from jax.experimental import pallas as pl
from jax.experimental.pallas import tpu as pltpu
from jax.sharding import PartitionSpec as P

MESH = pl.DeviceIdType.MESH
BF = jnp.bfloat16
F32 = jnp.float32


def flip(v, k):
    if k == 0:
        return v
    if k == 1:
        return v + 1 - 2 * (v % 2)
    if k == 2:
        return (v + 2) % 4
    return 3 - v


class Slots:
    def __init__(self):
        self.n = 0

    def take(self, k):
        first = self.n
        self.n += k
        return first


SLOTS = Slots()
ZA = SLOTS.take(4)
XP = SLOTS.take(4)
XM = SLOTS.take(4)
XF = SLOTS.take(4)
CA = SLOTS.take(4)
YH = SLOTS.take(4)
YR = SLOTS.take(4)
ZB = SLOTS.take(2)
ZR = SLOTS.take(1)
ZG = SLOTS.take(5)
YG = SLOTS.take(4)
YF = SLOTS.take(2)
GZ = SLOTS.take(2)
GY = SLOTS.take(3)
GF = SLOTS.take(1)
QC = SLOTS.take(1)
QX = SLOTS.take(1)
QZ = SLOTS.take(1)
FZ = SLOTS.take(1)
FX = SLOTS.take(1)
FC = SLOTS.take(1)
LEFT, RIGHT = pl.ds(0, 512), pl.ds(512, 384)


def rows(start, size):
    return pl.ds(pl.multiple_of(start, size), size)


def kernel(
    act, basis, og, gbasis, out,
    a, w, own, part, yl, yr, ysl, ysr, r1, s1, s1b, zbl, zbr, zsl, zsr, r2, g,
    ogv, gb, q, rc, q1, q1b, rx, q2, q2b, rz, fg, fgt, sq, sent,
    lsem, ssem, rsem,
):
    r, c = lax.axis_index("row"), lax.axis_index("col")
    y, zh = r // 4, r % 4
    zl, x, core = c // 8, (c // 2) % 4, c % 2
    half = a.shape[1] // 2

    def at(yy=y, zz=zh, ll=zl, xx=x, cc=core):
        return (yy * 4 + zz, ll * 8 + xx * 2 + cc)

    xp, xm = (x + 1) % 4, (x + 3) % 4
    yp, ym = (y + 1) % 4, (y + 3) % 4
    zp, zm = (zh + 1) % 4, (zh + 3) % 4
    mate = 1 - core

    def copy(src, dst, slot, dev):
        return pltpu.make_async_remote_copy(
            src_ref=src,
            dst_ref=dst,
            send_sem=ssem.at[0],
            recv_sem=rsem.at[slot],
            device_id=dev,
            device_id_type=MESH,
        )

    def send(src, dst, slot, dev):
        copy(src, dst, slot, dev).start()

    def arrived(like, slot):
        copy(like, like, slot, at(cc=mate)).wait_recv()

    load_act = pltpu.make_async_copy(act, a.at[rows(16 * c, 16)], lsem.at[0])
    load_og = pltpu.make_async_copy(og, ogv.at[rows(32 * r, 32)], lsem.at[1])
    load_w = pltpu.make_async_copy(basis, w, lsem.at[2])
    load_gb = pltpu.make_async_copy(gbasis, gb, lsem.at[3])
    load_act.start()
    load_og.start()
    load_gb.start()
    load_w.start()

    barrier = pltpu.get_barrier_semaphore()
    partners = [at(cc=mate)]
    for k in (1, 2, 3):
        partners += [at(ll=flip(zl, k)), at(xx=flip(x, k)), at(yy=flip(y, k))]
    partners += [at(zz=zp), at(zz=zm)]
    for dev in partners:
        pl.semaphore_signal(barrier, inc=1, device_id=dev, device_id_type=MESH)
    pl.semaphore_wait(barrier, len(partners))

    def piece(j, xx, cc):
        return rows(128 * flip(zl, j) + 32 * xx + 16 * cc, 16)

    near = (x, xm, xp, (x + 2) % 4)

    def xsend(j):
        p = a.at[piece(j, x, core)]
        send(p, p, XP + j, at(xx=xp))
        send(p, p, XM + j, at(xx=xm))

    def csend(j, i):
        p = a.at[piece(j, near[i], core)]
        send(p, p, CA + j, at(cc=mate))

    def zrecv(j):
        arrived(a.at[piece(j, x, core)], ZA + j)
        xsend(j)
        csend(j, 0)

    def xforward(j):
        p = piece(j, xm, core)
        arrived(a.at[p], XP + j)
        h = a.at[p, pl.ds(0, half)]
        send(h, h, XF + j, at(xx=xp))
        csend(j, 1)
        p = piece(j, xp, core)
        arrived(a.at[p], XM + j)
        h = a.at[p, pl.ds(half, half)]
        send(h, h, XF + j, at(xx=xm))
        csend(j, 2)

    def xfinish(j):
        arrived(a.at[piece(j, near[3], core)], XF + j)
        csend(j, 3)

    def sub(j, yy):
        return rows(128 * flip(zl, j) + 32 * yy, 32)

    def multiply(j):
        arrived(a.at[pl.ds(0, 64)], CA + j)
        block = rows(128 * flip(zl, j), 128)
        acc = jnp.dot(a[block, :], w[...], preferred_element_type=F32)
        own[block, :] = acc
        part[block, :] = acc.astype(BF)
        far = sub(j, (y + 2) % 4)
        send(part.at[far, LEFT], yl.at[j], YH + j, at(yy=ym))
        send(part.at[far, RIGHT], yr.at[j], YH + j, at(yy=yp))
        send(part.at[sub(j, yp), LEFT], r1.at[j, 1, :, LEFT], YR + j, at(yy=yp))
        send(part.at[sub(j, ym), RIGHT], r1.at[j, 0, :, RIGHT], YR + j, at(yy=ym))

    def addsend(j):
        arrived(r1.at[j, 0], YH + j)
        ysr[j] = (own[sub(j, yp), RIGHT] + yr[j].astype(F32)).astype(BF)
        send(ysr.at[j], r1.at[j, 1, :, RIGHT], YR + j, at(yy=yp))
        ysl[j] = (own[sub(j, ym), LEFT] + yl[j].astype(F32)).astype(BF)
        send(ysl.at[j], r1.at[j, 0, :, LEFT], YR + j, at(yy=ym))

    def owner(j):
        return (flip(zl, j) - zh + 4) % 4

    def ysum(j):
        arrived(r1.at[j], YR + j)
        total = own[sub(j, y), :] + r1[j, 0].astype(F32) + r1[j, 1].astype(F32)
        s1[j] = total
        s1b[j] = total.astype(BF)
        m = owner(j)

        @pl.when(m == 2)
        def _():
            send(s1b.at[j, :, LEFT], zbl, ZB + 0, at(zz=zm))
            send(s1b.at[j, :, RIGHT], zbr, ZB + 1, at(zz=zp))

        @pl.when(m == 1)
        def _():
            send(s1b.at[j, :, LEFT], r2.at[1, :, LEFT], ZR, at(zz=zp))

        @pl.when(m == 3)
        def _():
            send(s1b.at[j, :, RIGHT], r2.at[0, :, RIGHT], ZR, at(zz=zm))

    def zadd(j):
        m = owner(j)

        @pl.when(m == 1)
        def _():
            arrived(zbr, ZB + 1)
            zsr[...] = (s1[j, :, RIGHT] + zbr[...].astype(F32)).astype(BF)
            send(zsr, r2.at[1, :, RIGHT], ZR, at(zz=zp))

        @pl.when(m == 3)
        def _():
            arrived(zbl, ZB + 0)
            zsl[...] = (s1[j, :, LEFT] + zbl[...].astype(F32)).astype(BF)
            send(zsl, r2.at[0, :, LEFT], ZR, at(zz=zm))

    def ysend(j):
        lo, hi = g.at[sub(j, y), LEFT], g.at[sub(j, y), RIGHT]
        send(lo, lo, YG + j, at(yy=yp))
        send(hi, hi, YG + j, at(yy=ym))
        send(hi, hi, YF + j // 2, at(yy=yp))
        send(lo, lo, YF + j // 2, at(yy=ym))

    def yforward(j):
        arrived(g.at[pl.ds(0, 32)], YG + j)
        h = g.at[sub(j, ym), LEFT]
        send(h, h, YF + j // 2, at(yy=yp))
        h = g.at[sub(j, yp), RIGHT]
        send(h, h, YF + j // 2, at(yy=ym))

    def gsend(j, side, slot, dev):
        h = g.at[sub(j, y), side]
        send(h, h, ZG + slot, at(zz=dev))

    def round_own(j):
        @pl.when(owner(j) == 0)
        def _():
            arrived(r2, ZR)
            total = s1[j] + r2[0].astype(F32) + r2[1].astype(F32)
            g[sub(j, y), :] = total.astype(BF)
            gsend(j, LEFT, 0, zp)
            gsend(j, RIGHT, 1, zm)
            gsend(j, RIGHT, 2, zp)
            gsend(j, LEFT, 3, zm)
            ysend(j)

    def take_near(j):
        m = owner(j)

        @pl.when(m == 3)
        def _():
            arrived(g.at[sub(j, y), LEFT], ZG + 0)
            gsend(j, LEFT, 4, zp)
            arrived(g.at[sub(j, y), RIGHT], ZG + 2)
            ysend(j)

        @pl.when(m == 1)
        def _():
            arrived(g.at[sub(j, y), RIGHT], ZG + 1)
            gsend(j, RIGHT, 4, zm)
            arrived(g.at[sub(j, y), LEFT], ZG + 3)
            ysend(j)

    def take_far(j):
        @pl.when(owner(j) == 2)
        def _():
            arrived(g.at[sub(j, y)], ZG + 4)
            ysend(j)

    def forward_own(j):
        @pl.when(owner(j) == 0)
        def _():
            yforward(j)

    def forward_near(j):
        @pl.when(owner(j) % 2 == 1)
        def _():
            yforward(j)

    def forward_far(j):
        @pl.when(owner(j) == 2)
        def _():
            yforward(j)

    zring = (zh, zm, zp, (zh + 2) % 4)

    def gz(i, yy=y):
        return ogv.at[rows(128 * yy + 32 * zring[i], 32)]

    def gz_half(i, lower, yy=y):
        return ogv.at[rows(128 * yy + 32 * zring[i] + 16 * lower, 16)]

    def g_y(i, slot):
        send(gz(i), gz(i), GY + slot, at(yy=yp))
        send(gz(i), gz(i), GY + slot, at(yy=ym))

    def g_yforward(pieces, slot):
        arrived(ogv.at[pl.ds(0, 64 * len(pieces))], GY + slot)
        for i in pieces:
            h = gz_half(i, 0, ym)
            send(h, h, GF, at(yy=yp))
            h = gz_half(i, 1, yp)
            send(h, h, GF, at(yy=ym))

    def g_near():
        arrived(ogv.at[pl.ds(0, 64)], GZ + 0)
        h = gz_half(1, 0)
        send(h, h, GZ + 1, at(zz=zp))
        h = gz_half(2, 1)
        send(h, h, GZ + 1, at(zz=zm))
        g_y(1, 1)
        g_y(2, 1)

    def g_far():
        arrived(ogv.at[pl.ds(0, 32)], GZ + 1)
        g_y(3, 2)

    def q_core():
        arrived(ogv.at[pl.ds(0, 128)], GF)
        load_gb.wait()
        q[...] = jnp.dot(ogv[...], gb[...], preferred_element_type=F32).reshape(q.shape)
        send(q.at[:, mate], rc, QC, at(cc=mate))

    def q_x():
        arrived(rc, QC)
        v = (q[:, core] + rc[...]).reshape(q1.shape)
        q1[...] = v
        q1b[...] = v.astype(BF)
        for k in (1, 2, 3):
            send(q1b.at[:, flip(x, k)], rx.at[k - 1], QX, at(xx=flip(x, k)))

    def q_z():
        arrived(rx, QX)
        v = q1[:, x]
        for k in (1, 2, 3):
            v = v + rx[k - 1].astype(F32)
        q2[...] = v
        q2b[...] = v.astype(BF)
        for k in (1, 2, 3):
            send(q2b.at[flip(zl, k)], rz.at[k - 1], QZ, at(ll=flip(zl, k)))

    def f_z():
        arrived(rz, QZ)
        p = fg.at[zl, x, core]
        p[...] = (q2[zl] + rz[0].astype(F32) + rz[1].astype(F32) + rz[2].astype(F32)).astype(BF)
        for k in (1, 2, 3):
            send(p, p, FZ, at(ll=flip(zl, k)))

    def f_x():
        arrived(fg.at[0, pl.ds(0, 3), 0], FZ)
        p = fg.at[:, x, core]
        for k in (1, 2, 3):
            send(p, p, FX, at(xx=flip(x, k)))

    def f_core():
        arrived(fg.at[pl.ds(0, 3), :, 0], FX)
        p = fg.at[:, :, core]
        send(p, p, FC, at(cc=mate))

    def f_done():
        arrived(fg.at[:, :, mate], FC)
        fgt[...] = fg[...].reshape(fgt.shape[1], fgt.shape[0]).T

    load_og.wait()
    send(gz(0), gz(0), GZ + 0, at(zz=zp))
    send(gz(0), gz(0), GZ + 0, at(zz=zm))
    load_act.wait()
    p = a.at[rows(16 * c, 16)]
    for k in (1, 2, 3):
        send(p, p, ZA + k, at(ll=flip(zl, k)))
    xsend(0)
    csend(0, 0)

    g_y(0, 0)
    zrecv(1)
    xforward(0)
    zrecv(2)
    g_near()
    zrecv(3)
    xforward(1)
    xfinish(0)
    g_yforward((0,), 0)
    xforward(2)
    xfinish(1)
    xforward(3)
    g_far()
    load_w.wait()
    multiply(0)
    xfinish(2)
    g_yforward((1, 2), 1)
    multiply(1)
    addsend(0)
    xfinish(3)
    g_yforward((3,), 2)
    multiply(2)
    addsend(1)
    multiply(3)
    q_core()
    ysum(0)
    addsend(2)
    q_x()
    ysum(1)
    addsend(3)
    ysum(2)
    zadd(0)
    ysum(3)
    zadd(1)
    q_z()
    zadd(2)
    zadd(3)
    round_own(0)
    round_own(1)
    round_own(2)
    forward_own(0)
    round_own(3)
    f_z()
    forward_own(1)
    take_near(0)
    forward_own(2)
    take_near(1)
    forward_own(3)
    f_x()
    take_near(2)
    forward_near(0)
    take_near(3)
    forward_near(1)
    take_far(0)
    take_far(1)
    forward_near(2)
    f_core()
    take_far(2)
    forward_near(3)
    forward_far(0)
    take_far(3)
    forward_far(1)
    f_done()
    forward_far(2)
    forward_far(3)

    mine = 256 * (zl // 2)
    other = 256 - mine
    cuts = [pl.ds(256 * i, min(256, g.shape[1] - 256 * i)) for i in range(4)]
    arrived(g.at[pl.ds(0, 128)], YF + 0)
    for cut in cuts:
        s = jnp.dot(fgt[:, rows(mine, 256)], g[rows(mine, 256), cut], preferred_element_type=F32)
        sq[:, cut] = s * s
    arrived(g.at[pl.ds(0, 128)], YF + 1)
    for cut in cuts:
        s = jnp.dot(fgt[:, rows(other, 256)], g[rows(other, 256), cut], preferred_element_type=F32)
        out[:, cut] = ((sq[:, cut] + s * s) * 0.5).astype(BF)

    copy(sent, sent, 0, at(cc=mate)).wait_send()


def solution(mesh):
    def local(activations, act_basis, out_grads, grad_basis):
        nin, nout = act_basis.shape[1], grad_basis.shape[1]
        tok = 512
        apiece, gpiece = 2 * activations.size, 2 * 32 * nin
        opiece, fpiece = 2 * out_grads.size, 2 * 16 * nout
        sent = (
            (3 + 4 * 3 + 16) * apiece
            + (4 * 3 + 3 + 3 + 4 * 3) * gpiece
            + (3 + 3 * 4) * opiece
            + (2 * 16 + 3 * 4 + 3) * fpiece
            + (3 + 3 * 4 + 16) * fpiece
        )
        any_ = pl.BlockSpec(memory_space=pl.ANY)
        v = pltpu.VMEM
        return pl.pallas_call(
            kernel,
            out_shape=pltpu.VMEM((nout, nin), BF),
            in_specs=[any_] * 4,
            out_specs=pl.BlockSpec(memory_space=pltpu.VMEM),
            scratch_shapes=[
                v((tok, act_basis.shape[0]), BF),
                v(act_basis.shape, BF),
                v((tok, nin), F32),
                v((tok, nin), BF),
                v((4, 32, 512), BF),
                v((4, 32, 384), BF),
                v((4, 32, 512), BF),
                v((4, 32, 384), BF),
                v((4, 2, 32, nin), BF),
                v((4, 32, nin), F32),
                v((4, 32, nin), BF),
                v((32, 512), BF),
                v((32, 384), BF),
                v((32, 512), BF),
                v((32, 384), BF),
                v((2, 32, nin), BF),
                v((tok, nin), BF),
                v((tok, out_grads.shape[1]), BF),
                v(grad_basis.shape, BF),
                v((16, 2, 16, nout), F32),
                v((16, 16, nout), F32),
                v((4, 4, 16, nout), F32),
                v((4, 4, 16, nout), BF),
                v((3, 4, 16, nout), BF),
                v((4, 16, nout), F32),
                v((4, 16, nout), BF),
                v((3, 16, nout), BF),
                v((4, 4, 2, 16, nout), BF),
                v((nout, tok), BF),
                v((nout, nin), F32),
                v((sent // 256, 128), BF),
                pltpu.SemaphoreType.DMA((4,)),
                pltpu.SemaphoreType.DMA((1,)),
                pltpu.SemaphoreType.DMA((SLOTS.n,)),
            ],
            compiler_params=pltpu.CompilerParams(
                collective_id=0, has_side_effects=True
            ),
        )(activations, act_basis, out_grads, grad_basis)

    return jax.shard_map(
        local,
        mesh=mesh,
        in_specs=(P("col", "row"), P("row", "col"), P("row", "col"), P("col", "row")),
        out_specs=P("row", "col"),
        check_vma=False,
    )
```

```python
import jax
import jax.numpy as jnp
from jax import lax
from jax.experimental import pallas as pl
from jax.experimental.pallas import tpu as pltpu
from jax.sharding import PartitionSpec as P

MESH = pl.DeviceIdType.MESH
BF = jnp.bfloat16
F32 = jnp.float32


def flip(v, k):
    if k == 0:
        return v
    if k == 1:
        return v + 1 - 2 * (v % 2)
    if k == 2:
        return (v + 2) % 4
    return 3 - v


class Slots:
    def __init__(self):
        self.n = 0

    def take(self, k):
        first = self.n
        self.n += k
        return first


SLOTS = Slots()
ZA = SLOTS.take(4)
XP = SLOTS.take(4)
XM = SLOTS.take(4)
XF = SLOTS.take(4)
CA = SLOTS.take(4)
YH = SLOTS.take(4)
YR = SLOTS.take(4)
ZB = SLOTS.take(2)
ZR = SLOTS.take(1)
ZG = SLOTS.take(5)
YG = SLOTS.take(4)
YF = SLOTS.take(2)
GZ = SLOTS.take(2)
GY = SLOTS.take(3)
GF = SLOTS.take(1)
QC = SLOTS.take(1)
QX = SLOTS.take(1)
QZ = SLOTS.take(1)
FZ = SLOTS.take(1)
FX = SLOTS.take(1)
FC = SLOTS.take(1)
LEFT, RIGHT = pl.ds(0, 512), pl.ds(512, 384)


def rows(start, size):
    return pl.ds(pl.multiple_of(start, size), size)


def kernel(
    act, basis, og, gbasis, out,
    a, w, own, part, yl, yr, ysl, ysr, r1, s1, s1b, zbl, zbr, zsl, zsr, r2, g,
    ogv, gb, q, rc, q1, q1b, rx, q2, q2b, rz, fg, fgt, sq, sent,
    lsem, ssem, rsem,
):
    r, c = lax.axis_index("row"), lax.axis_index("col")
    y, zh = r // 4, r % 4
    zl, x, core = c // 8, (c // 2) % 4, c % 2
    half = a.shape[1] // 2

    def at(yy=y, zz=zh, ll=zl, xx=x, cc=core):
        return (yy * 4 + zz, ll * 8 + xx * 2 + cc)

    xp, xm = (x + 1) % 4, (x + 3) % 4
    yp, ym = (y + 1) % 4, (y + 3) % 4
    zp, zm = (zh + 1) % 4, (zh + 3) % 4
    mate = 1 - core

    def copy(src, dst, slot, dev):
        return pltpu.make_async_remote_copy(
            src_ref=src,
            dst_ref=dst,
            send_sem=ssem.at[0],
            recv_sem=rsem.at[slot],
            device_id=dev,
            device_id_type=MESH,
        )

    def send(src, dst, slot, dev):
        copy(src, dst, slot, dev).start()

    def arrived(like, slot):
        copy(like, like, slot, at(cc=mate)).wait_recv()

    load_act = pltpu.make_async_copy(act, a.at[rows(16 * c, 16)], lsem.at[0])
    load_og = pltpu.make_async_copy(og, ogv.at[rows(32 * r, 32)], lsem.at[1])
    load_w = pltpu.make_async_copy(basis, w, lsem.at[2])
    load_gb = pltpu.make_async_copy(gbasis, gb, lsem.at[3])
    load_act.start()
    load_og.start()
    load_gb.start()
    load_w.start()

    barrier = pltpu.get_barrier_semaphore()
    partners = [at(cc=mate)]
    for k in (1, 2, 3):
        partners += [at(ll=flip(zl, k)), at(xx=flip(x, k)), at(yy=flip(y, k))]
    partners += [at(zz=zp), at(zz=zm)]
    for dev in partners:
        pl.semaphore_signal(barrier, inc=1, device_id=dev, device_id_type=MESH)
    pl.semaphore_wait(barrier, len(partners))

    def piece(j, xx, cc):
        return rows(128 * flip(zl, j) + 32 * xx + 16 * cc, 16)

    near = (x, xm, xp, (x + 2) % 4)

    def xsend(j):
        p = a.at[piece(j, x, core)]
        send(p, p, XP + j, at(xx=xp))
        send(p, p, XM + j, at(xx=xm))

    def csend(j, i):
        p = a.at[piece(j, near[i], core)]
        send(p, p, CA + j, at(cc=mate))

    def zrecv(j):
        arrived(a.at[piece(j, x, core)], ZA + j)
        xsend(j)
        csend(j, 0)

    def xforward(j):
        p = piece(j, xm, core)
        arrived(a.at[p], XP + j)
        h = a.at[p, pl.ds(0, half)]
        send(h, h, XF + j, at(xx=xp))
        csend(j, 1)
        p = piece(j, xp, core)
        arrived(a.at[p], XM + j)
        h = a.at[p, pl.ds(half, half)]
        send(h, h, XF + j, at(xx=xm))
        csend(j, 2)

    def xfinish(j):
        arrived(a.at[piece(j, near[3], core)], XF + j)
        csend(j, 3)

    def sub(j, yy):
        return rows(128 * flip(zl, j) + 32 * yy, 32)

    def multiply(j):
        arrived(a.at[pl.ds(0, 64)], CA + j)
        block = rows(128 * flip(zl, j), 128)
        acc = jnp.dot(a[block, :], w[...], preferred_element_type=F32)
        own[block, :] = acc
        part[block, :] = acc.astype(BF)
        far = sub(j, (y + 2) % 4)
        send(part.at[far, LEFT], yl.at[j], YH + j, at(yy=ym))
        send(part.at[far, RIGHT], yr.at[j], YH + j, at(yy=yp))
        send(part.at[sub(j, yp), LEFT], r1.at[j, 1, :, LEFT], YR + j, at(yy=yp))
        send(part.at[sub(j, ym), RIGHT], r1.at[j, 0, :, RIGHT], YR + j, at(yy=ym))

    def addsend(j):
        arrived(r1.at[j, 0], YH + j)
        ysr[j] = (own[sub(j, yp), RIGHT] + yr[j].astype(F32)).astype(BF)
        send(ysr.at[j], r1.at[j, 1, :, RIGHT], YR + j, at(yy=yp))
        ysl[j] = (own[sub(j, ym), LEFT] + yl[j].astype(F32)).astype(BF)
        send(ysl.at[j], r1.at[j, 0, :, LEFT], YR + j, at(yy=ym))

    def owner(j):
        return (flip(zl, j) - zh + 4) % 4

    def ysum(j):
        arrived(r1.at[j], YR + j)
        total = own[sub(j, y), :] + r1[j, 0].astype(F32) + r1[j, 1].astype(F32)
        s1[j] = total
        s1b[j] = total.astype(BF)
        m = owner(j)

        @pl.when(m == 2)
        def _():
            send(s1b.at[j, :, LEFT], zbl, ZB + 0, at(zz=zm))
            send(s1b.at[j, :, RIGHT], zbr, ZB + 1, at(zz=zp))

        @pl.when(m == 1)
        def _():
            send(s1b.at[j, :, LEFT], r2.at[1, :, LEFT], ZR, at(zz=zp))

        @pl.when(m == 3)
        def _():
            send(s1b.at[j, :, RIGHT], r2.at[0, :, RIGHT], ZR, at(zz=zm))

    def zadd(j):
        m = owner(j)

        @pl.when(m == 1)
        def _():
            arrived(zbr, ZB + 1)
            zsr[...] = (s1[j, :, RIGHT] + zbr[...].astype(F32)).astype(BF)
            send(zsr, r2.at[1, :, RIGHT], ZR, at(zz=zp))

        @pl.when(m == 3)
        def _():
            arrived(zbl, ZB + 0)
            zsl[...] = (s1[j, :, LEFT] + zbl[...].astype(F32)).astype(BF)
            send(zsl, r2.at[0, :, LEFT], ZR, at(zz=zm))

    def ysend(j):
        lo, hi = g.at[sub(j, y), LEFT], g.at[sub(j, y), RIGHT]
        send(lo, lo, YG + j, at(yy=yp))
        send(hi, hi, YG + j, at(yy=ym))
        send(hi, hi, YF + j // 2, at(yy=yp))
        send(lo, lo, YF + j // 2, at(yy=ym))

    def yforward(j):
        arrived(g.at[pl.ds(0, 32)], YG + j)
        h = g.at[sub(j, ym), LEFT]
        send(h, h, YF + j // 2, at(yy=yp))
        h = g.at[sub(j, yp), RIGHT]
        send(h, h, YF + j // 2, at(yy=ym))

    def gsend(j, side, slot, dev):
        h = g.at[sub(j, y), side]
        send(h, h, ZG + slot, at(zz=dev))

    def round_own(j):
        @pl.when(owner(j) == 0)
        def _():
            arrived(r2, ZR)
            total = s1[j] + r2[0].astype(F32) + r2[1].astype(F32)
            g[sub(j, y), :] = total.astype(BF)
            gsend(j, LEFT, 0, zp)
            gsend(j, RIGHT, 1, zm)
            gsend(j, RIGHT, 2, zp)
            gsend(j, LEFT, 3, zm)
            ysend(j)

    def take_near(j):
        m = owner(j)

        @pl.when(m == 3)
        def _():
            arrived(g.at[sub(j, y), LEFT], ZG + 0)
            gsend(j, LEFT, 4, zp)
            arrived(g.at[sub(j, y), RIGHT], ZG + 2)
            ysend(j)

        @pl.when(m == 1)
        def _():
            arrived(g.at[sub(j, y), RIGHT], ZG + 1)
            gsend(j, RIGHT, 4, zm)
            arrived(g.at[sub(j, y), LEFT], ZG + 3)
            ysend(j)

    def take_far(j):
        @pl.when(owner(j) == 2)
        def _():
            arrived(g.at[sub(j, y)], ZG + 4)
            ysend(j)

    def forward_own(j):
        @pl.when(owner(j) == 0)
        def _():
            yforward(j)

    def forward_near(j):
        @pl.when(owner(j) % 2 == 1)
        def _():
            yforward(j)

    def forward_far(j):
        @pl.when(owner(j) == 2)
        def _():
            yforward(j)

    zring = (zh, zm, zp, (zh + 2) % 4)

    def gz(i, yy=y):
        return ogv.at[rows(128 * yy + 32 * zring[i], 32)]

    def gz_half(i, lower, yy=y):
        return ogv.at[rows(128 * yy + 32 * zring[i] + 16 * lower, 16)]

    def g_y(i, slot):
        send(gz(i), gz(i), GY + slot, at(yy=yp))
        send(gz(i), gz(i), GY + slot, at(yy=ym))

    def g_yforward(pieces, slot):
        arrived(ogv.at[pl.ds(0, 64 * len(pieces))], GY + slot)
        for i in pieces:
            h = gz_half(i, 0, ym)
            send(h, h, GF, at(yy=yp))
            h = gz_half(i, 1, yp)
            send(h, h, GF, at(yy=ym))

    def g_near():
        arrived(ogv.at[pl.ds(0, 64)], GZ + 0)
        h = gz_half(1, 0)
        send(h, h, GZ + 1, at(zz=zp))
        h = gz_half(2, 1)
        send(h, h, GZ + 1, at(zz=zm))
        g_y(1, 1)
        g_y(2, 1)

    def g_far():
        arrived(ogv.at[pl.ds(0, 32)], GZ + 1)
        g_y(3, 2)

    def q_core():
        arrived(ogv.at[pl.ds(0, 128)], GF)
        load_gb.wait()
        q[...] = jnp.dot(ogv[...], gb[...], preferred_element_type=F32).reshape(q.shape)
        send(q.at[:, mate], rc, QC, at(cc=mate))

    def q_x():
        arrived(rc, QC)
        v = (q[:, core] + rc[...]).reshape(q1.shape)
        q1[...] = v
        q1b[...] = v.astype(BF)
        for k in (1, 2, 3):
            send(q1b.at[:, flip(x, k)], rx.at[k - 1], QX, at(xx=flip(x, k)))

    def q_z():
        arrived(rx, QX)
        v = q1[:, x]
        for k in (1, 2, 3):
            v = v + rx[k - 1].astype(F32)
        q2[...] = v
        q2b[...] = v.astype(BF)
        for k in (1, 2, 3):
            send(q2b.at[flip(zl, k)], rz.at[k - 1], QZ, at(ll=flip(zl, k)))

    def f_z():
        arrived(rz, QZ)
        p = fg.at[zl, x, core]
        p[...] = (q2[zl] + rz[0].astype(F32) + rz[1].astype(F32) + rz[2].astype(F32)).astype(BF)
        for k in (1, 2, 3):
            send(p, p, FZ, at(ll=flip(zl, k)))

    def f_x():
        arrived(fg.at[0, pl.ds(0, 3), 0], FZ)
        p = fg.at[:, x, core]
        for k in (1, 2, 3):
            send(p, p, FX, at(xx=flip(x, k)))

    def f_core():
        arrived(fg.at[pl.ds(0, 3), :, 0], FX)
        p = fg.at[:, :, core]
        send(p, p, FC, at(cc=mate))

    def f_done():
        arrived(fg.at[:, :, mate], FC)
        fgt[...] = fg[...].reshape(fgt.shape[1], fgt.shape[0]).T

    load_og.wait()
    send(gz(0), gz(0), GZ + 0, at(zz=zp))
    send(gz(0), gz(0), GZ + 0, at(zz=zm))
    load_act.wait()
    p = a.at[rows(16 * c, 16)]
    for k in (1, 2, 3):
        send(p, p, ZA + k, at(ll=flip(zl, k)))
    xsend(0)
    csend(0, 0)

    g_y(0, 0)
    zrecv(1)
    xforward(0)
    g_near()
    zrecv(2)
    zrecv(3)
    xforward(1)
    xfinish(0)
    g_yforward((0,), 0)
    xforward(2)
    xfinish(1)
    xforward(3)
    g_far()
    load_w.wait()
    multiply(0)
    xfinish(2)
    g_yforward((1, 2), 1)
    multiply(1)
    addsend(0)
    xfinish(3)
    g_yforward((3,), 2)
    multiply(2)
    addsend(1)
    multiply(3)
    q_core()
    ysum(0)
    addsend(2)
    q_x()
    ysum(1)
    addsend(3)
    ysum(2)
    zadd(0)
    ysum(3)
    zadd(1)
    q_z()
    zadd(2)
    zadd(3)
    round_own(0)
    round_own(1)
    round_own(2)
    forward_own(0)
    round_own(3)
    f_z()
    forward_own(1)
    take_near(0)
    forward_own(2)
    take_near(1)
    forward_own(3)
    f_x()
    take_near(2)
    forward_near(0)
    take_near(3)
    forward_near(1)
    take_far(0)
    take_far(1)
    forward_near(2)
    f_core()
    take_far(2)
    forward_near(3)
    forward_far(0)
    take_far(3)
    forward_far(1)
    f_done()
    forward_far(2)
    forward_far(3)

    mine = 256 * (zl // 2)
    other = 256 - mine
    cuts = [pl.ds(256 * i, min(256, g.shape[1] - 256 * i)) for i in range(4)]
    arrived(g.at[pl.ds(0, 128)], YF + 0)
    for cut in cuts:
        s = jnp.dot(fgt[:, rows(mine, 256)], g[rows(mine, 256), cut], preferred_element_type=F32)
        sq[:, cut] = s * s
    arrived(g.at[pl.ds(0, 128)], YF + 1)
    for cut in cuts:
        s = jnp.dot(fgt[:, rows(other, 256)], g[rows(other, 256), cut], preferred_element_type=F32)
        out[:, cut] = ((sq[:, cut] + s * s) * 0.5).astype(BF)

    copy(sent, sent, 0, at(cc=mate)).wait_send()


def solution(mesh):
    def local(activations, act_basis, out_grads, grad_basis):
        nin, nout = act_basis.shape[1], grad_basis.shape[1]
        tok = 512
        apiece, gpiece = 2 * activations.size, 2 * 32 * nin
        opiece, fpiece = 2 * out_grads.size, 2 * 16 * nout
        sent = (
            (3 + 4 * 3 + 16) * apiece
            + (4 * 3 + 3 + 3 + 4 * 3) * gpiece
            + (3 + 3 * 4) * opiece
            + (2 * 16 + 3 * 4 + 3) * fpiece
            + (3 + 3 * 4 + 16) * fpiece
        )
        any_ = pl.BlockSpec(memory_space=pl.ANY)
        v = pltpu.VMEM
        return pl.pallas_call(
            kernel,
            out_shape=pltpu.VMEM((nout, nin), BF),
            in_specs=[any_] * 4,
            out_specs=pl.BlockSpec(memory_space=pltpu.VMEM),
            scratch_shapes=[
                v((tok, act_basis.shape[0]), BF),
                v(act_basis.shape, BF),
                v((tok, nin), F32),
                v((tok, nin), BF),
                v((4, 32, 512), BF),
                v((4, 32, 384), BF),
                v((4, 32, 512), BF),
                v((4, 32, 384), BF),
                v((4, 2, 32, nin), BF),
                v((4, 32, nin), F32),
                v((4, 32, nin), BF),
                v((32, 512), BF),
                v((32, 384), BF),
                v((32, 512), BF),
                v((32, 384), BF),
                v((2, 32, nin), BF),
                v((tok, nin), BF),
                v((tok, out_grads.shape[1]), BF),
                v(grad_basis.shape, BF),
                v((16, 2, 16, nout), F32),
                v((16, 16, nout), F32),
                v((4, 4, 16, nout), F32),
                v((4, 4, 16, nout), BF),
                v((3, 4, 16, nout), BF),
                v((4, 16, nout), F32),
                v((4, 16, nout), BF),
                v((3, 16, nout), BF),
                v((4, 4, 2, 16, nout), BF),
                v((nout, tok), BF),
                v((nout, nin), F32),
                v((sent // 256, 128), BF),
                pltpu.SemaphoreType.DMA((4,)),
                pltpu.SemaphoreType.DMA((1,)),
                pltpu.SemaphoreType.DMA((SLOTS.n,)),
            ],
            compiler_params=pltpu.CompilerParams(
                collective_id=0, has_side_effects=True
            ),
        )(activations, act_basis, out_grads, grad_basis)

    return jax.shard_map(
        local,
        mesh=mesh,
        in_specs=(P("col", "row"), P("row", "col"), P("row", "col"), P("col", "row")),
        out_specs=P("row", "col"),
        check_vma=False,
    )
```
